32 devices in a mesh: row: 8 (over z, y), col: 4 (over x, core).
Axes of the slice: x: 2, y: 2, z: 4, core: 2. Of those that a mesh axis runs over, the one named last changes fastest.
Arguments:
- pair_rep: bfloat16 [1024, 1024, 128], P('row', 'col'), may hold values from -8 to 8
- row_ids: int32 [16], P('row'), may hold values from 0 to 1023, as said below
- pad_mask: int32 [1024], P('col'), may hold values from 0 to 1, as said below
- ln_gain: float32 [128], replicated, may hold values from 0.25 to 1.75
- ln_bias: float32 [128], replicated, may hold values from -2 to 2
- w_query: bfloat16 [128, 128], replicated, may hold values from -2 to 2
- w_key: bfloat16 [128, 128], replicated, may hold values from -2 to 2
- w_value: bfloat16 [128, 128], replicated, may hold values from -0.5 to 0.5
- w_gate: bfloat16 [128, 128], replicated, may hold values from -0.5 to 0.5
- gate_bias: float32 [128], replicated, may hold values from -4 to 4
- w_bias: bfloat16 [128, 4], replicated, may hold values from -0.5 to 0.5
- w_out: bfloat16 [128, 128], replicated, may hold values from -0.5 to 0.5
Outputs:
- update: bfloat16 [16, 1024, 128], P('col', 'row')
The draws below stay inside these ranges and needn't reach their ends.
Inputs may be any that keep to these rules, and one draw needn't show every extreme that they name: `row_ids`: entries t * 2 to t * 2 + 1 are distinct and lie in [t * 128, (t + 1) * 128). `pad_mask`: A prefix of the tokens is real and the rest is padding; the first 257 tokens are real.
All inputs are finite; a program needn't handle non-finite values.
Results may differ from the reference program's by a relative error of at most 0.023.
Values may be sent and summed in bfloat16 or wider, within the bound.
A program may use at most 128 MiB of HBM per device.

```python
import math
import jax
import jax.numpy as jnp
from jax import lax

CZ = 128
HEADS = 4
HEAD_DIM = 32
ROW_BLOCK = 128
ROWS_DEV = 2
TOKENS = 1024
SELECTED = 16


def draw_row_ids(key, part):
    groups = SELECTED // ROWS_DEV
    keys = jax.random.split(jax.random.fold_in(key, 11), groups)
    picks = jax.vmap(lambda single: jax.random.permutation(single, ROW_BLOCK)[:ROWS_DEV])(keys)
    picks = picks + (jnp.arange(groups, dtype=jnp.int32) * ROW_BLOCK)[:, None]
    return picks.reshape(-1).astype(jnp.int32)


def draw_pad_mask(key, part):
    length = jax.random.randint(jax.random.fold_in(key, 23), (), TOKENS // 4 + 1, TOKENS + 1)
    return (jnp.arange(TOKENS, dtype=jnp.int32) < length).astype(jnp.int32)


def unit_direction(key):
    raw = jnp.clip(jax.random.normal(jax.random.fold_in(key, 101), (CZ,), jnp.float32), -3.0, 3.0)
    raw = raw - jnp.mean(raw)
    return raw / jnp.sqrt(jnp.sum(raw * raw))


def head_vector(key):
    raw = jax.random.normal(jax.random.fold_in(key, 211), (HEADS, HEAD_DIM), jnp.float32)
    raw = raw / jnp.sqrt(jnp.sum(raw * raw, axis=1, keepdims=True))
    strength = 280.0 / CZ * (0.8 + 0.2 * jnp.arange(HEADS, dtype=jnp.float32) / max(HEADS - 1, 1))
    radius = jnp.sqrt(strength * math.sqrt(HEAD_DIM))
    return (raw * radius[:, None]).reshape(HEADS * HEAD_DIM)


def projection_weight(key, salt):
    direction = unit_direction(key)
    along = head_vector(key)
    sub = jax.random.fold_in(key, salt)
    base = jnp.clip(jax.random.normal(sub, (CZ, HEADS * HEAD_DIM), jnp.float32), -4.0, 4.0) / math.sqrt(CZ)
    return jnp.clip(base + direction[:, None] * along[None, :], -2.0, 2.0).astype(jnp.bfloat16)


def draw_w_query(key, part):
    return projection_weight(key, 41)


def draw_w_key(key, part):
    return projection_weight(key, 43)


def draw_ln_bias(key, part):
    direction = unit_direction(key)
    sub = jax.random.fold_in(key, 31)
    raw = jnp.clip(0.5 * jax.random.normal(sub, (CZ,), jnp.float32), -1.5, 1.5)
    return raw - jnp.sum(raw * direction) * direction


def noise_block(key, shape, direction):
    raw = jnp.clip(jax.random.normal(key, shape, jnp.float32), -4.0, 4.0)
    return raw - jnp.sum(raw * direction, axis=-1, keepdims=True) * direction


def draw_pair_rep(key, part):
    direction = unit_direction(key)
    base_key = jax.random.fold_in(key, 53)

    def one_block(index):
        sub = jax.random.fold_in(base_key, index)
        block = noise_block(sub, (TOKENS // 16, TOKENS, CZ), direction)
        return jnp.clip(block, -8.0, 8.0).astype(jnp.bfloat16)
    full = lax.map(one_block, jnp.arange(16, dtype=jnp.int32)).reshape(TOKENS, TOKENS, CZ)
    row_ids = draw_row_ids(key, part)
    count = 3
    picks = jax.random.permutation(jax.random.fold_in(key, 61), SELECTED)[:count]
    planted_rows = row_ids[picks]
    spots = jax.random.permutation(jax.random.fold_in(key, 67), TOKENS // 4)[:6]
    cosines = jnp.array([1.0, 0.993, 0.986, 0.8, 0.65, 0.5], jnp.float32)
    sines = jnp.sqrt(1.0 - cosines * cosines)
    extra = noise_block(jax.random.fold_in(key, 71), (count, 6, CZ), direction)
    planted = cosines[None, :, None] * math.sqrt(CZ) * direction[None, None, :] + sines[None, :, None] * extra
    planted = jnp.clip(planted, -8.0, 8.0).astype(jnp.bfloat16)
    return full.at[planted_rows[:, None], spots[None, :]].set(planted)


def noise(stream_key, extent, scale, limit, held_as=jnp.bfloat16):
    values = scale * jax.random.normal(stream_key, extent, jnp.float32)
    return jnp.clip(values, min=-limit, max=limit).astype(held_as)


def setup_inputs(seed: int = 0) -> dict:
    seeds = jax.random.split(jax.random.key(seed), 13)
    pair_rep = draw_pair_rep(jax.random.fold_in(seeds[12], 71), 0)
    row_ids = draw_row_ids(jax.random.fold_in(seeds[12], 71), 0)
    pad_mask = draw_pad_mask(jax.random.fold_in(seeds[12], 71), 0)
    ln_gain = jnp.clip(1.0 + 0.15 * jax.random.normal(seeds[3], (CZ,), jnp.float32), 0.25, 1.75)
    ln_bias = draw_ln_bias(jax.random.fold_in(seeds[12], 71), 0)
    w_query = draw_w_query(jax.random.fold_in(seeds[12], 71), 0)
    w_key = draw_w_key(jax.random.fold_in(seeds[12], 71), 0)
    w_value = noise(seeds[7], (CZ, HEADS * HEAD_DIM), CZ ** -0.5, 0.5)
    w_gate = noise(seeds[8], (CZ, HEADS * HEAD_DIM), CZ ** -0.5, 0.5)
    gate_bias = noise(seeds[9], (HEADS * HEAD_DIM,), 1.0, 4.0, jnp.float32)
    w_bias = noise(seeds[10], (CZ, HEADS), CZ ** -0.5, 0.5)
    w_out = noise(seeds[11], (HEADS * HEAD_DIM, CZ), (HEADS * HEAD_DIM) ** -0.5, 0.5)
    return dict(pair_rep=pair_rep, row_ids=row_ids, pad_mask=pad_mask, ln_gain=ln_gain, ln_bias=ln_bias, w_query=w_query, w_key=w_key, w_value=w_value, w_gate=w_gate, gate_bias=gate_bias, w_bias=w_bias, w_out=w_out)


def layer_norm(values, ln_gain, ln_bias):
    values = values.astype(jnp.float32)
    centre = lax.optimization_barrier(jnp.mean(values, axis=-1, keepdims=True))
    spread = lax.optimization_barrier(jnp.mean((values - centre) ** 2, axis=-1, keepdims=True))
    return ((values - centre) * lax.rsqrt(spread + 1e-05) * ln_gain + ln_bias).astype(jnp.bfloat16)

def project(normed, weight):
    flat = normed.reshape(-1, normed.shape[-1])
    return jnp.dot(flat, weight, preferred_element_type=jnp.float32).reshape(normed.shape[:-1] + (weight.shape[1],))

def reference(pair_rep, row_ids, pad_mask, ln_gain, ln_bias, w_query, w_key, w_value, w_gate, gate_bias, w_bias, w_out):
    tokens = pair_rep.shape[0]
    heads = w_bias.shape[1]
    width = w_query.shape[1]
    head_dim = width // heads
    block_count = tokens // 16

    def bias_block(block):
        normed = layer_norm(block, ln_gain, ln_bias)
        return jnp.einsum('jkc,ch->hjk', normed.astype(jnp.float32), w_bias.astype(jnp.float32))
    blocks = pair_rep.reshape(block_count, tokens // block_count, tokens, pair_rep.shape[2])
    pair_bias = lax.map(bias_block, blocks)
    pair_bias = jnp.transpose(pair_bias, (1, 0, 2, 3)).reshape(heads, tokens, tokens)
    chosen = layer_norm(pair_rep[row_ids.astype(jnp.int32)], ln_gain, ln_bias)
    query = (project(chosen, w_query) / jnp.sqrt(jnp.float32(head_dim))).astype(jnp.bfloat16)
    key_rows = project(chosen, w_key).astype(jnp.bfloat16)
    value_rows = project(chosen, w_value).astype(jnp.bfloat16)
    gate = jax.nn.sigmoid(project(chosen, w_gate) + gate_bias).astype(jnp.bfloat16)
    key_live = pad_mask > 0

    def attend_row(items):
        query_row, key_row, value_row = items
        query_heads = query_row.reshape(tokens, heads, head_dim).astype(jnp.float32)
        key_heads = key_row.reshape(tokens, heads, head_dim).astype(jnp.float32)
        value_heads = value_row.reshape(tokens, heads, head_dim).astype(jnp.float32)
        scores = jnp.einsum('jhd,khd->hjk', query_heads, key_heads) + pair_bias
        scores = jnp.where(key_live[None, None, :], scores, jnp.float32(-1000000000.0))
        peak = lax.optimization_barrier(jnp.max(scores, axis=-1, keepdims=True))
        expo = jnp.exp(scores - peak)
        totals = lax.optimization_barrier(jnp.sum(expo, axis=-1))
        probs = expo.astype(jnp.bfloat16).astype(jnp.float32)
        summed = jnp.einsum('hjk,khd->hjd', probs, value_heads) / totals[..., None]
        return jnp.transpose(summed, (1, 0, 2)).reshape(tokens, width)
    attended = lax.map(attend_row, (query, key_rows, value_rows))
    gated = (gate.astype(jnp.float32) * attended).astype(jnp.bfloat16)
    return project(gated, w_out).astype(jnp.bfloat16)
```

```python
import functools
import jax
import jax.numpy as jnp
from jax import lax
from jax.experimental import pallas as pl
from jax.experimental.pallas import tpu as pltpu
from jax.sharding import PartitionSpec as P

F32 = jnp.float32
BF16 = jnp.bfloat16
VM = pl.BlockSpec(memory_space=pltpu.VMEM)
ROWS_CHUNK = 16
ROWS_STEP = 8


def norm_kernel(ids, x_ref, gain_ref, shift_ref, o_ref):
    x = x_ref[0].astype(F32)
    centre = jnp.mean(x, axis=-1, keepdims=True)
    d = x - centre
    spread = jnp.mean(d * d, axis=-1, keepdims=True)
    o_ref[0] = (d * lax.rsqrt(spread + 1e-05) * gain_ref[...] + shift_ref[...]).astype(BF16)


def chosen_normed(pair_rep, offsets, gain, shift):
    rows, cols, cz = pair_rep.shape
    return pl.pallas_call(
        norm_kernel,
        out_shape=jax.ShapeDtypeStruct((offsets.shape[0], cols, cz), BF16),
        grid_spec=pltpu.PrefetchScalarGridSpec(
            num_scalar_prefetch=1,
            grid=(offsets.shape[0],),
            in_specs=[
                pl.BlockSpec((1, cols, cz), lambda i, ids: (ids[i], 0, 0)),
                pl.BlockSpec((1, cz), lambda i, ids: (0, 0)),
                pl.BlockSpec((1, cz), lambda i, ids: (0, 0)),
            ],
            out_specs=pl.BlockSpec((1, cols, cz), lambda i, ids: (i, 0, 0)),
        ),
    )(offsets, pair_rep, gain, shift)


def main_kernel(
    cfg,
    pair_ref, nloc, mask_ref, left_ref, add_ref, wq_ref, wkv_ref, wg_ref, gb_ref, wo_ref,
    out_ref,
    xbuf, rbuf, bias, nall, qn, osend, orecv, lsel, msel, strans, srecv,
    xsem, own_sem, ring_send, ring_recv, q_send, q_recv, o_send, o_recv, s_send, s_recv,
):
    n_row, n_col, rows, cols, cz, heads, rows_dev, selected = cfg
    head_dim = cz // heads
    per = selected // n_col
    half = n_row // 2
    first_half = rows_dev // 2
    MESH = pl.DeviceIdType.MESH
    r = lax.axis_index("row")
    c = lax.axis_index("col")

    def row_of(pos):
        pos = lax.rem(pos + 2 * n_row, n_row)
        return jnp.where(pos < half, 2 * pos, 2 * (n_row - 1 - pos) + 1)

    odd = lax.rem(r, 2)
    pos = jnp.where(odd == 0, r // 2, n_row - 1 - r // 2)
    nexts = (row_of(pos + 1), row_of(pos - 1))
    root = (r * rows) // cols
    start = pl.multiple_of(lax.rem(r * rows, cols), rows)
    is_root = c == root

    def x_copy(k):
        where = pl.ds(k * ROWS_CHUNK, ROWS_CHUNK)
        return pltpu.make_async_copy(pair_ref.at[where], xbuf.at[where], xsem.at[k])

    chunks = rows // ROWS_CHUNK
    for k in range(chunks):
        x_copy(k).start()
    own = pltpu.make_async_copy(nloc, nall.at[pl.ds(r * rows_dev, rows_dev)], own_sem)
    own.start()

    barrier = pltpu.get_barrier_semaphore()
    for nb in nexts:
        pl.semaphore_signal(barrier, inc=1, device_id=(nb, c), device_id_type=MESH)
    for dc in range(1, n_col):
        pl.semaphore_signal(
            barrier, inc=1, device_id=(r, lax.rem(c + dc, n_col)), device_id_type=MESH
        )
    pl.semaphore_wait(barrier, 2 + n_col - 1)

    def valid(way, s, u):
        if s < half:
            return True
        return s == half and ((u < first_half) if way == 0 else (u >= first_half))

    def ring(way, s, u):
        origin = row_of(pos - (s - 1) if way == 0 else pos + (s - 1))
        t = origin * rows_dev + u
        return pltpu.make_async_remote_copy(
            src_ref=nloc.at[u] if s == 1 else nall.at[t],
            dst_ref=nall.at[t],
            send_sem=ring_send.at[way],
            recv_sem=ring_recv.at[way, s - 1, u],
            device_id=(nexts[way], c),
            device_id_type=MESH,
        )

    def q_local(t):
        return pltpu.make_async_copy(nall.at[t, pl.ds(start, rows)], qn.at[t], q_recv.at[t])

    def q_remote(t, dc):
        return pltpu.make_async_remote_copy(
            src_ref=nall.at[t, pl.ds(start, rows)],
            dst_ref=qn.at[t],
            send_sem=q_send.at[dc - 1],
            recv_sem=q_recv.at[t],
            device_id=(r, lax.rem(c + dc, n_col)),
            device_id_type=MESH,
        )

    def q_share(t):
        @pl.when(is_root)
        def _():
            for dc in range(1, n_col):
                q_remote(t, dc).start()
            q_local(t).start()

    for u in range(rows_dev):
        for way in (0, 1):
            ring(way, 1, u).start()
    own.wait()
    for u in range(rows_dev):
        q_share(r * rows_dev + u)

    events = [
        [(way, s, u) for way in (0, 1) if valid(way, s, u)]
        for s in range(1, half + 1)
        for u in range(rows_dev)
    ]

    def arrive(way, s, u):
        t = row_of(pos - s if way == 0 else pos + s) * rows_dev + u
        pltpu.make_async_remote_copy(
            src_ref=nall.at[t],
            dst_ref=nall.at[t],
            send_sem=ring_send.at[way],
            recv_sem=ring_recv.at[way, s - 1, u],
            device_id=(nexts[way], c),
            device_id_type=MESH,
        ).wait_recv()
        if valid(way, s + 1, u):
            ring(way, s + 1, u).start()
        q_share(t)

    row_i = lax.broadcasted_iota(jnp.int32, (cz, cz), 0)
    col_i = lax.broadcasted_iota(jnp.int32, (cz, cz), 1)
    centring = (jnp.where(row_i == col_i, 1.0, 0.0) - 1.0 / cz).astype(BF16)
    left = left_ref[...]

    def bias_step(j0):
        j0 = pl.multiple_of(j0, ROWS_STEP)
        x = xbuf[pl.ds(j0, ROWS_STEP)].reshape(ROWS_STEP * cols, cz)
        d = jnp.dot(x, centring, preferred_element_type=F32).astype(BF16)
        both = jnp.concatenate([d, d * d], axis=-1)
        res = lax.dot_general(
            left, both, (((1,), (1,)), ((), ())), preferred_element_type=F32
        )
        for jj in range(ROWS_STEP):
            at = pl.ds(pl.multiple_of((j0 + jj) * 16, 16), 16)
            for part in range(cols // 128):
                first = jj * cols + part * 128
                rbuf[part, at, :] = res[:, first : first + 128]

    for k in range(chunks):
        x_copy(k).wait()

        def one(b, _, k=k):
            bias_step(k * ROWS_CHUNK + b * ROWS_STEP)
            return 0

        lax.fori_loop(0, ROWS_CHUNK // ROWS_STEP, one, 0)
        lo = k * len(events) // chunks
        hi = (k + 1) * len(events) // chunks
        for group in events[lo:hi]:
            for way, s, u in group:
                arrive(way, s, u)

    for part in range(cols // 128):
        lanes = slice(part * 128, (part + 1) * 128)
        rstd = lax.rsqrt(rbuf[part, pl.ds(2 * heads, rows, stride=16), :] + 1e-05)
        live = mask_ref[:, lanes] > 0
        for h in range(heads):
            raw = (
                rbuf[part, pl.ds(h, rows, stride=16), :]
                + rbuf[part, pl.ds(heads + h, rows, stride=16), :]
            )
            full = raw * rstd + add_ref[h]
            bias[pl.ds(h * rows, rows), lanes] = jnp.where(live, full, F32(-1e9))

    lane = lax.broadcasted_iota(jnp.int32, (rows, cz), 1)
    in_head = [(lane // head_dim) == h for h in range(heads)]
    ones = jnp.ones((cols, cz), BF16)
    lsel[...] = jnp.ones_like(lsel)
    msel[...] = jnp.zeros_like(msel)
    scale = F32(1.0 / (head_dim ** 0.5))

    def o_copy(t, peer):
        return pltpu.make_async_remote_copy(
            src_ref=osend.at[t],
            dst_ref=orecv.at[c, lax.rem(t, per)],
            send_sem=o_send.at[peer],
            recv_sem=o_recv.at[c],
            device_id=(r, peer),
            device_id_type=MESH,
        )

    def attend(t):
        q_local(t).wait()
        kv = jnp.dot(nall[t], wkv_ref[...], preferred_element_type=F32).astype(BF16)
        key = kv[:, :cz]
        value = jnp.concatenate([kv[:, cz:], ones], axis=-1)
        q = (jnp.dot(qn[t], wq_ref[...], preferred_element_type=F32) * scale).astype(BF16)
        q4 = jnp.concatenate([jnp.where(in_head[h], q, jnp.zeros_like(q)) for h in range(heads)], 0)
        s = lax.dot_general(q4, key, (((1,), (1,)), ((), ())), preferred_element_type=F32)
        s = s + bias[...]
        m = jnp.max(s, axis=-1, keepdims=True)
        p = jnp.exp(s - m).astype(BF16)
        o = jnp.dot(p, value, preferred_element_type=F32)
        num = jnp.zeros((rows, cz), F32)
        den = jnp.zeros((rows, cz), F32)
        ls = lsel[...]
        ms = msel[...]
        for h in range(heads):
            oh = o[h * rows : (h + 1) * rows, :cz]
            lh = o[h * rows : (h + 1) * rows, cz:]
            num = jnp.where(in_head[h], oh, num)
            den = jnp.where(in_head[h], lh, den)
            here = lane == t * heads + h
            ls = jnp.where(here, lh, ls)
            ms = jnp.where(here, m[h * rows : (h + 1) * rows], ms)
        lsel[...] = ls
        msel[...] = ms
        osend[t] = (num / den).astype(BF16)

    for dc in range(1, n_col):
        peer = lax.rem(c + dc, n_col)

        def step(i, _, peer=peer):
            t = peer * per + i
            attend(t)
            o_copy(t, peer).start()
            return 0

        lax.fori_loop(0, per, step, 0)

    def step_own(i, _):
        attend(c * per + i)
        return 0

    lax.fori_loop(0, per, step_own, 0)

    strans[...] = jnp.transpose(msel[...] + jnp.log(lsel[...]))
    ph = per * heads

    def s_copy(peer):
        return pltpu.make_async_remote_copy(
            src_ref=strans.at[pl.ds(pl.multiple_of(peer * ph, 8), ph)],
            dst_ref=srecv.at[pl.ds(pl.multiple_of(c * ph, 8), ph)],
            send_sem=s_send.at[peer],
            recv_sem=s_recv.at[c],
            device_id=(r, peer),
            device_id_type=MESH,
        )

    for dc in range(1, n_col):
        s_copy(lax.rem(c + dc, n_col)).start()
    own_rows = pl.ds(pl.multiple_of(c * ph, 8), ph)
    srecv[own_rows, :] = strans[own_rows, :]

    gates = []
    for i in range(per):
        g = jnp.dot(qn[c * per + i], wg_ref[...], preferred_element_type=F32) + gb_ref[...]
        gates.append(jax.nn.sigmoid(g).astype(BF16).astype(F32))
    span = selected * heads
    er = lax.broadcasted_iota(jnp.int32, (span, n_col * per * cz), 0)
    ec = lax.broadcasted_iota(jnp.int32, (span, n_col * per * cz), 1)
    expand = jnp.where(er == ec // head_dim, 1.0, 0.0).astype(BF16)

    for dc in range(1, n_col):
        src = lax.rem(c + dc, n_col)
        pltpu.make_async_remote_copy(
            src_ref=strans.at[pl.ds(0, ph)],
            dst_ref=srecv.at[pl.ds(pl.multiple_of(src * ph, 8), ph)],
            send_sem=s_send.at[src],
            recv_sem=s_recv.at[src],
            device_id=(r, src),
            device_id_type=MESH,
        ).wait_recv()
    stats = [srecv[pl.ds(k * ph, ph), :] for k in range(n_col)]
    top = functools.reduce(jnp.maximum, stats)
    weights = [jnp.exp(a - top) for a in stats]
    total = functools.reduce(jnp.add, weights)
    parts = jnp.concatenate([w / total for w in weights], axis=0)
    spread_w = jnp.dot(jnp.transpose(parts).astype(BF16), expand, preferred_element_type=F32)

    for dc in range(1, n_col):
        src = lax.rem(c + dc, n_col)
        pltpu.make_async_remote_copy(
            src_ref=osend.at[pl.ds(0, per)],
            dst_ref=orecv.at[src],
            send_sem=o_send.at[src],
            recv_sem=o_recv.at[src],
            device_id=(r, src),
            device_id_type=MESH,
        ).wait_recv()
    for i in range(per):
        orecv[c, i] = osend[c * per + i]
    for i in range(per):
        acc = jnp.zeros((rows, cz), F32)
        for k in range(n_col):
            at = (k * per + i) * cz
            acc = acc + spread_w[:, at : at + cz] * orecv[k, i].astype(F32)
        gated = (gates[i] * acc).astype(BF16)
        out_ref[i] = jnp.dot(gated, wo_ref[...], preferred_element_type=F32).astype(BF16)

    for dc in range(1, n_col):
        peer = lax.rem(c + dc, n_col)
        s_copy(peer).wait_send()
        pltpu.make_async_remote_copy(
            src_ref=osend.at[pl.ds(0, per)],
            dst_ref=orecv.at[c],
            send_sem=o_send.at[peer],
            recv_sem=o_recv.at[c],
            device_id=(r, peer),
            device_id_type=MESH,
        ).wait_send()

        @pl.when(is_root)
        def _(dc=dc):
            pltpu.make_async_remote_copy(
                src_ref=qn,
                dst_ref=qn,
                send_sem=q_send.at[dc - 1],
                recv_sem=q_recv.at[0],
                device_id=(r, lax.rem(c + dc, n_col)),
                device_id_type=MESH,
            ).wait_send()

    for way in (0, 1):
        count = sum(valid(way, s, u) for s in range(1, half + 1) for u in range(rows_dev))
        pltpu.make_async_remote_copy(
            src_ref=nall.at[pl.ds(0, count)],
            dst_ref=nall.at[pl.ds(0, count)],
            send_sem=ring_send.at[way],
            recv_sem=ring_recv.at[way, 0, 0],
            device_id=(nexts[way], c),
            device_id_type=MESH,
        ).wait_send()


def body(
    pair_rep, row_ids, pad_mask, ln_gain, ln_bias, w_query, w_key, w_value, w_gate, gate_bias,
    w_bias, w_out,
):
    rows, cols, cz = pair_rep.shape
    heads = w_bias.shape[1]
    n_row = lax.axis_size("row")
    n_col = lax.axis_size("col")
    rows_dev = row_ids.shape[0]
    selected = rows_dev * n_row
    per = selected // n_col
    half = n_row // 2
    offsets = row_ids - lax.axis_index("row") * rows
    nloc = chosen_normed(pair_rep, offsets, ln_gain[None], ln_bias[None])
    scaled = (ln_gain[:, None] * w_bias.astype(F32)).T
    high = scaled.astype(BF16)
    low = (scaled - high.astype(F32)).astype(BF16)
    zero = jnp.zeros_like(high)
    left = jnp.concatenate(
        [
            jnp.concatenate([high, zero], 1),
            jnp.concatenate([low, zero], 1),
            jnp.concatenate([jnp.zeros((1, cz), BF16), jnp.full((1, cz), 1.0 / cz, BF16)], 1),
            jnp.zeros((16 - 2 * heads - 1, 2 * cz), BF16),
        ],
        0,
    )
    add = jnp.sum(ln_bias[:, None] * w_bias.astype(F32), axis=0)
    cfg = (n_row, n_col, rows, cols, cz, heads, rows_dev, selected)
    DMA = pltpu.SemaphoreType.DMA
    return pl.pallas_call(
        functools.partial(main_kernel, cfg),
        out_shape=jax.ShapeDtypeStruct((per, rows, cz), BF16),
        in_specs=[pl.BlockSpec(memory_space=pl.ANY), VM, VM, VM,
                  pl.BlockSpec(memory_space=pltpu.SMEM), VM, VM, VM, VM, VM],
        out_specs=VM,
        scratch_shapes=[
            pltpu.VMEM((rows, cols, cz), BF16),
            pltpu.VMEM((cols // 128, rows * 16, 128), F32),
            pltpu.VMEM((heads * rows, cols), F32),
            pltpu.VMEM((selected, cols, cz), BF16),
            pltpu.VMEM((selected, rows, cz), BF16),
            pltpu.VMEM((selected, rows, cz), BF16),
            pltpu.VMEM((n_col, per, rows, cz), BF16),
            pltpu.VMEM((rows, cz), F32),
            pltpu.VMEM((rows, cz), F32),
            pltpu.VMEM((cz, rows), F32),
            pltpu.VMEM((selected * heads, rows), F32),
            DMA((rows // ROWS_CHUNK,)),
            DMA,
            DMA((2,)),
            DMA((2, half, rows_dev)),
            DMA((n_col - 1,)),
            DMA((selected,)),
            DMA((n_col,)),
            DMA((n_col,)),
            DMA((n_col,)),
            DMA((n_col,)),
        ],
        compiler_params=pltpu.CompilerParams(
            collective_id=0, has_side_effects=True, vmem_limit_bytes=56 * 2**20
        ),
    )(
        pair_rep, nloc, pad_mask[None], left, add, w_query,
        jnp.concatenate([w_key, w_value], axis=1), w_gate, gate_bias[None], w_out,
    )


def solution(mesh):
    return jax.shard_map(
        body,
        mesh=mesh,
        in_specs=(P("row", "col", None), P("row"), P("col")) + (P(),) * 9,
        out_specs=P("col", "row", None),
        check_vma=False,
    )
```

```python
import functools
import jax
import jax.numpy as jnp
from jax import lax
from jax.experimental import pallas as pl
from jax.experimental.pallas import tpu as pltpu
from jax.sharding import PartitionSpec as P

F32 = jnp.float32
BF16 = jnp.bfloat16
VM = pl.BlockSpec(memory_space=pltpu.VMEM)
ROWS_CHUNK = 16
ROWS_STEP = 8


def norm_kernel(ids, x_ref, gain_ref, shift_ref, o_ref):
    x = x_ref[0].astype(F32)
    centre = jnp.mean(x, axis=-1, keepdims=True)
    d = x - centre
    spread = jnp.mean(d * d, axis=-1, keepdims=True)
    o_ref[0] = (d * lax.rsqrt(spread + 1e-05) * gain_ref[...] + shift_ref[...]).astype(BF16)


def chosen_normed(pair_rep, offsets, gain, shift):
    rows, cols, cz = pair_rep.shape
    return pl.pallas_call(
        norm_kernel,
        out_shape=jax.ShapeDtypeStruct((offsets.shape[0], cols, cz), BF16),
        grid_spec=pltpu.PrefetchScalarGridSpec(
            num_scalar_prefetch=1,
            grid=(offsets.shape[0],),
            in_specs=[
                pl.BlockSpec((1, cols, cz), lambda i, ids: (lax.rem(ids[i], rows), 0, 0)),
                pl.BlockSpec((1, cz), lambda i, ids: (0, 0)),
                pl.BlockSpec((1, cz), lambda i, ids: (0, 0)),
            ],
            out_specs=pl.BlockSpec((1, cols, cz), lambda i, ids: (i, 0, 0)),
        ),
    )(offsets, pair_rep, gain, shift)


def main_kernel(
    cfg,
    pair_ref, nloc, mask_ref, gain_ref, shift_ref, wb_ref, wq_ref, wk_ref, wv_ref, wg_ref, gb_ref,
    wo_ref,
    out_ref,
    xbuf, rbuf, bias, nall, qn, osend, orecv, lsel, msel, strans, srecv,
    xsem, own_sem, ring_send, ring_recv, q_send, q_recv, o_send, o_recv, s_send, s_recv,
):
    n_row, n_col, rows, cols, cz, heads, rows_dev, selected = cfg
    head_dim = cz // heads
    per = selected // n_col
    half = n_row // 2
    first_half = rows_dev // 2
    MESH = pl.DeviceIdType.MESH
    r = lax.axis_index("row")
    c = lax.axis_index("col")

    def row_of(pos):
        pos = lax.rem(pos + 2 * n_row, n_row)
        return jnp.where(pos < half, 2 * pos, 2 * (n_row - 1 - pos) + 1)

    odd = lax.rem(r, 2)
    pos = jnp.where(odd == 0, r // 2, n_row - 1 - r // 2)
    nexts = (row_of(pos + 1), row_of(pos - 1))
    root = (r * rows) // cols
    start = pl.multiple_of(lax.rem(r * rows, cols), rows)
    is_root = c == root

    def x_copy(k):
        where = pl.ds(k * ROWS_CHUNK, ROWS_CHUNK)
        return pltpu.make_async_copy(pair_ref.at[where], xbuf.at[where], xsem.at[k])

    chunks = rows // ROWS_CHUNK
    for k in range(chunks):
        x_copy(k).start()
    own = pltpu.make_async_copy(nloc, nall.at[pl.ds(r * rows_dev, rows_dev)], own_sem)
    own.start()

    barrier = pltpu.get_barrier_semaphore()
    for nb in nexts:
        pl.semaphore_signal(barrier, inc=1, device_id=(nb, c), device_id_type=MESH)
    for dc in range(1, n_col):
        pl.semaphore_signal(
            barrier, inc=1, device_id=(r, lax.rem(c + dc, n_col)), device_id_type=MESH
        )
    pl.semaphore_wait(barrier, 2 + n_col - 1)

    def valid(way, s, u):
        if s < half:
            return True
        return s == half and ((u < first_half) if way == 0 else (u >= first_half))

    def ring(way, s, u):
        origin = row_of(pos - (s - 1) if way == 0 else pos + (s - 1))
        t = origin * rows_dev + u
        return pltpu.make_async_remote_copy(
            src_ref=nloc.at[u] if s == 1 else nall.at[t],
            dst_ref=nall.at[t],
            send_sem=ring_send.at[way],
            recv_sem=ring_recv.at[way, s - 1, u],
            device_id=(nexts[way], c),
            device_id_type=MESH,
        )

    def q_local(t):
        return pltpu.make_async_copy(nall.at[t, pl.ds(start, rows)], qn.at[t], q_recv.at[t])

    def q_remote(t, dc):
        return pltpu.make_async_remote_copy(
            src_ref=nall.at[t, pl.ds(start, rows)],
            dst_ref=qn.at[t],
            send_sem=q_send.at[dc - 1],
            recv_sem=q_recv.at[t],
            device_id=(r, lax.rem(c + dc, n_col)),
            device_id_type=MESH,
        )

    def q_share(t):
        @pl.when(is_root)
        def _():
            for dc in range(1, n_col):
                q_remote(t, dc).start()
            q_local(t).start()

    for u in range(rows_dev):
        for way in (0, 1):
            ring(way, 1, u).start()
    own.wait()
    for u in range(rows_dev):
        q_share(r * rows_dev + u)

    events = [
        [(way, s, u) for way in (0, 1) if valid(way, s, u)]
        for s in range(1, half + 1)
        for u in range(rows_dev)
    ]

    def arrive(way, s, u):
        t = row_of(pos - s if way == 0 else pos + s) * rows_dev + u
        pltpu.make_async_remote_copy(
            src_ref=nall.at[t],
            dst_ref=nall.at[t],
            send_sem=ring_send.at[way],
            recv_sem=ring_recv.at[way, s - 1, u],
            device_id=(nexts[way], c),
            device_id_type=MESH,
        ).wait_recv()
        if valid(way, s + 1, u):
            ring(way, s + 1, u).start()
        q_share(t)

    row_i = lax.broadcasted_iota(jnp.int32, (cz, cz), 0)
    col_i = lax.broadcasted_iota(jnp.int32, (cz, cz), 1)
    centring = (jnp.where(row_i == col_i, 1.0, 0.0) - 1.0 / cz).astype(BF16)
    pick = lax.broadcasted_iota(jnp.int32, (16, heads), 0)
    head_i = lax.broadcasted_iota(jnp.int32, (16, heads), 1)
    pick = jnp.where((pick == head_i) | (pick == head_i + heads), 1.0, 0.0).astype(BF16)
    by_head = lax.dot_general(
        pick, wb_ref[...], (((1,), (0,)), ((), ())), preferred_element_type=F32
    )
    add = jnp.sum(by_head * shift_ref[...], axis=-1, keepdims=True)
    scaled = by_head * gain_ref[...]
    high = scaled.astype(BF16).astype(F32)
    line = lax.broadcasted_iota(jnp.int32, (16, cz), 0)
    left = jnp.concatenate(
        [
            jnp.where(line < heads, high, scaled - high),
            jnp.where(line == 2 * heads, F32(1.0 / cz), F32(0.0)),
        ],
        axis=-1,
    ).astype(BF16)

    def bias_step(j0):
        j0 = pl.multiple_of(j0, ROWS_STEP)
        x = xbuf[pl.ds(j0, ROWS_STEP)].reshape(ROWS_STEP * cols, cz)
        d = jnp.dot(x, centring, preferred_element_type=F32).astype(BF16)
        both = jnp.concatenate([d, d * d], axis=-1)
        res = lax.dot_general(
            left, both, (((1,), (1,)), ((), ())), preferred_element_type=F32
        )
        for jj in range(ROWS_STEP):
            at = pl.ds(pl.multiple_of((j0 + jj) * 16, 16), 16)
            for part in range(cols // 128):
                first = jj * cols + part * 128
                rbuf[part, at, :] = res[:, first : first + 128]

    for k in range(chunks):
        x_copy(k).wait()

        def one(b, _, k=k):
            bias_step(k * ROWS_CHUNK + b * ROWS_STEP)
            return 0

        lax.fori_loop(0, ROWS_CHUNK // ROWS_STEP, one, 0)
        lo = k * len(events) // chunks
        hi = (k + 1) * len(events) // chunks
        for group in events[lo:hi]:
            for way, s, u in group:
                arrive(way, s, u)

    for part in range(cols // 128):
        lanes = slice(part * 128, (part + 1) * 128)
        rstd = lax.rsqrt(rbuf[part, pl.ds(2 * heads, rows, stride=16), :] + 1e-05)
        live = mask_ref[:, lanes] > 0
        for h in range(heads):
            raw = (
                rbuf[part, pl.ds(h, rows, stride=16), :]
                + rbuf[part, pl.ds(heads + h, rows, stride=16), :]
            )
            full = raw * rstd + add[h : h + 1]
            bias[pl.ds(h * rows, rows), lanes] = jnp.where(live, full, F32(-1e9))

    lane = lax.broadcasted_iota(jnp.int32, (rows, cz), 1)
    in_head = [(lane // head_dim) == h for h in range(heads)]
    ones = jnp.ones((cols, cz), BF16)
    wkv = jnp.concatenate([wk_ref[...], wv_ref[...]], axis=-1)
    lsel[...] = jnp.ones_like(lsel)
    msel[...] = jnp.zeros_like(msel)
    scale = F32(1.0 / (head_dim ** 0.5))

    def o_copy(t, peer):
        return pltpu.make_async_remote_copy(
            src_ref=osend.at[t],
            dst_ref=orecv.at[c, lax.rem(t, per)],
            send_sem=o_send.at[peer],
            recv_sem=o_recv.at[c],
            device_id=(r, peer),
            device_id_type=MESH,
        )

    def attend(t):
        q_local(t).wait()
        kv = jnp.dot(nall[t], wkv, preferred_element_type=F32).astype(BF16)
        key = kv[:, :cz]
        value = jnp.concatenate([kv[:, cz:], ones], axis=-1)
        q = (jnp.dot(qn[t], wq_ref[...], preferred_element_type=F32) * scale).astype(BF16)
        q4 = jnp.concatenate([jnp.where(in_head[h], q, jnp.zeros_like(q)) for h in range(heads)], 0)
        s = lax.dot_general(q4, key, (((1,), (1,)), ((), ())), preferred_element_type=F32)
        s = s + bias[...]
        m = jnp.max(s, axis=-1, keepdims=True)
        p = jnp.exp(s - m).astype(BF16)
        o = jnp.dot(p, value, preferred_element_type=F32)
        num = jnp.zeros((rows, cz), F32)
        den = jnp.zeros((rows, cz), F32)
        ls = lsel[...]
        ms = msel[...]
        for h in range(heads):
            oh = o[h * rows : (h + 1) * rows, :cz]
            lh = o[h * rows : (h + 1) * rows, cz:]
            num = jnp.where(in_head[h], oh, num)
            den = jnp.where(in_head[h], lh, den)
            here = lane == t * heads + h
            ls = jnp.where(here, lh, ls)
            ms = jnp.where(here, m[h * rows : (h + 1) * rows], ms)
        lsel[...] = ls
        msel[...] = ms
        osend[t] = (num / den).astype(BF16)

    for dc in range(1, n_col):
        peer = lax.rem(c + dc, n_col)

        def step(i, _, peer=peer):
            t = peer * per + i
            attend(t)
            o_copy(t, peer).start()
            return 0

        lax.fori_loop(0, per, step, 0)

    def step_own(i, _):
        attend(c * per + i)
        return 0

    lax.fori_loop(0, per, step_own, 0)

    strans[...] = jnp.transpose(msel[...] + jnp.log(lsel[...]))
    ph = per * heads

    def s_copy(peer):
        return pltpu.make_async_remote_copy(
            src_ref=strans.at[pl.ds(pl.multiple_of(peer * ph, 8), ph)],
            dst_ref=srecv.at[pl.ds(pl.multiple_of(c * ph, 8), ph)],
            send_sem=s_send.at[peer],
            recv_sem=s_recv.at[c],
            device_id=(r, peer),
            device_id_type=MESH,
        )

    for dc in range(1, n_col):
        s_copy(lax.rem(c + dc, n_col)).start()
    own_rows = pl.ds(pl.multiple_of(c * ph, 8), ph)
    srecv[own_rows, :] = strans[own_rows, :]

    gates = []
    for i in range(per):
        g = jnp.dot(qn[c * per + i], wg_ref[...], preferred_element_type=F32) + gb_ref[...]
        gates.append(jax.nn.sigmoid(g).astype(BF16).astype(F32))
    span = selected * heads
    er = lax.broadcasted_iota(jnp.int32, (span, n_col * per * cz), 0)
    ec = lax.broadcasted_iota(jnp.int32, (span, n_col * per * cz), 1)
    expand = jnp.where(er == ec // head_dim, 1.0, 0.0).astype(BF16)

    for dc in range(1, n_col):
        src = lax.rem(c + dc, n_col)
        pltpu.make_async_remote_copy(
            src_ref=strans.at[pl.ds(0, ph)],
            dst_ref=srecv.at[pl.ds(pl.multiple_of(src * ph, 8), ph)],
            send_sem=s_send.at[src],
            recv_sem=s_recv.at[src],
            device_id=(r, src),
            device_id_type=MESH,
        ).wait_recv()
    stats = [srecv[pl.ds(k * ph, ph), :] for k in range(n_col)]
    top = functools.reduce(jnp.maximum, stats)
    weights = [jnp.exp(a - top) for a in stats]
    total = functools.reduce(jnp.add, weights)
    parts = jnp.concatenate([w / total for w in weights], axis=0)
    spread_w = jnp.dot(jnp.transpose(parts).astype(BF16), expand, preferred_element_type=F32)

    for dc in range(1, n_col):
        src = lax.rem(c + dc, n_col)
        pltpu.make_async_remote_copy(
            src_ref=osend.at[pl.ds(0, per)],
            dst_ref=orecv.at[src],
            send_sem=o_send.at[src],
            recv_sem=o_recv.at[src],
            device_id=(r, src),
            device_id_type=MESH,
        ).wait_recv()
    for i in range(per):
        orecv[c, i] = osend[c * per + i]
    for i in range(per):
        acc = jnp.zeros((rows, cz), F32)
        for k in range(n_col):
            at = (k * per + i) * cz
            acc = acc + spread_w[:, at : at + cz] * orecv[k, i].astype(F32)
        gated = (gates[i] * acc).astype(BF16)
        out_ref[i] = jnp.dot(gated, wo_ref[...], preferred_element_type=F32).astype(BF16)

    for dc in range(1, n_col):
        peer = lax.rem(c + dc, n_col)
        s_copy(peer).wait_send()
        pltpu.make_async_remote_copy(
            src_ref=osend.at[pl.ds(0, per)],
            dst_ref=orecv.at[c],
            send_sem=o_send.at[peer],
            recv_sem=o_recv.at[c],
            device_id=(r, peer),
            device_id_type=MESH,
        ).wait_send()

        @pl.when(is_root)
        def _(dc=dc):
            pltpu.make_async_remote_copy(
                src_ref=qn,
                dst_ref=qn,
                send_sem=q_send.at[dc - 1],
                recv_sem=q_recv.at[0],
                device_id=(r, lax.rem(c + dc, n_col)),
                device_id_type=MESH,
            ).wait_send()

    for way in (0, 1):
        count = sum(valid(way, s, u) for s in range(1, half + 1) for u in range(rows_dev))
        pltpu.make_async_remote_copy(
            src_ref=nall.at[pl.ds(0, count)],
            dst_ref=nall.at[pl.ds(0, count)],
            send_sem=ring_send.at[way],
            recv_sem=ring_recv.at[way, 0, 0],
            device_id=(nexts[way], c),
            device_id_type=MESH,
        ).wait_send()


def body(
    pair_rep, row_ids, pad_mask, ln_gain, ln_bias, w_query, w_key, w_value, w_gate, gate_bias,
    w_bias, w_out,
):
    rows, cols, cz = pair_rep.shape
    heads = w_bias.shape[1]
    n_row = lax.axis_size("row")
    n_col = lax.axis_size("col")
    rows_dev = row_ids.shape[0]
    selected = rows_dev * n_row
    per = selected // n_col
    half = n_row // 2
    nloc = chosen_normed(pair_rep, row_ids, ln_gain[None], ln_bias[None])
    cfg = (n_row, n_col, rows, cols, cz, heads, rows_dev, selected)
    DMA = pltpu.SemaphoreType.DMA
    return pl.pallas_call(
        functools.partial(main_kernel, cfg),
        out_shape=jax.ShapeDtypeStruct((per, rows, cz), BF16),
        in_specs=[pl.BlockSpec(memory_space=pl.ANY)] + [VM] * 11,
        out_specs=VM,
        scratch_shapes=[
            pltpu.VMEM((rows, cols, cz), BF16),
            pltpu.VMEM((cols // 128, rows * 16, 128), F32),
            pltpu.VMEM((heads * rows, cols), F32),
            pltpu.VMEM((selected, cols, cz), BF16),
            pltpu.VMEM((selected, rows, cz), BF16),
            pltpu.VMEM((selected, rows, cz), BF16),
            pltpu.VMEM((n_col, per, rows, cz), BF16),
            pltpu.VMEM((rows, cz), F32),
            pltpu.VMEM((rows, cz), F32),
            pltpu.VMEM((cz, rows), F32),
            pltpu.VMEM((selected * heads, rows), F32),
            DMA((rows // ROWS_CHUNK,)),
            DMA,
            DMA((2,)),
            DMA((2, half, rows_dev)),
            DMA((n_col - 1,)),
            DMA((selected,)),
            DMA((n_col,)),
            DMA((n_col,)),
            DMA((n_col,)),
            DMA((n_col,)),
        ],
        compiler_params=pltpu.CompilerParams(
            collective_id=0, has_side_effects=True, vmem_limit_bytes=56 * 2**20
        ),
    )(
        pair_rep, nloc, pad_mask[None], ln_gain[None], ln_bias[None], w_bias.T, w_query, w_key,
        w_value, w_gate, gate_bias[None], w_out,
    )


def solution(mesh):
    return jax.shard_map(
        body,
        mesh=mesh,
        in_specs=(P("row", "col", None), P("row"), P("col")) + (P(),) * 9,
        out_specs=P("col", "row", None),
        check_vma=False,
    )
```

```python
import functools
import jax
import jax.numpy as jnp
from jax import lax
from jax.experimental import pallas as pl
from jax.experimental.pallas import tpu as pltpu
from jax.sharding import PartitionSpec as P

F32 = jnp.float32
BF16 = jnp.bfloat16
VM = pl.BlockSpec(memory_space=pltpu.VMEM)
ROWS_CHUNK = 16
ROWS_STEP = 16
PIECES = 1


def norm_kernel(ids, x_ref, gain_ref, shift_ref, o_ref):
    x = x_ref[0].astype(F32)
    centre = jnp.mean(x, axis=-1, keepdims=True)
    d = x - centre
    spread = jnp.mean(d * d, axis=-1, keepdims=True)
    o_ref[0] = (d * lax.rsqrt(spread + 1e-05) * gain_ref[...] + shift_ref[...]).astype(BF16)


def chosen_normed(pair_rep, offsets, gain, shift):
    rows, cols, cz = pair_rep.shape
    return pl.pallas_call(
        norm_kernel,
        out_shape=jax.ShapeDtypeStruct((offsets.shape[0], cols, cz), BF16),
        grid_spec=pltpu.PrefetchScalarGridSpec(
            num_scalar_prefetch=1,
            grid=(offsets.shape[0],),
            in_specs=[
                pl.BlockSpec((1, cols, cz), lambda i, ids: (lax.rem(ids[i], rows), 0, 0)),
                pl.BlockSpec((1, cz), lambda i, ids: (0, 0)),
                pl.BlockSpec((1, cz), lambda i, ids: (0, 0)),
            ],
            out_specs=pl.BlockSpec((1, cols, cz), lambda i, ids: (i, 0, 0)),
        ),
    )(offsets, pair_rep, gain, shift)


def main_kernel(
    cfg,
    pair_ref, nloc, mask_ref, gain_ref, shift_ref, wb_ref, wq_ref, wk_ref, wv_ref, wg_ref, gb_ref,
    wo_ref,
    out_ref,
    xbuf, rbuf, bias, nall, qn, osend, orecv, lsel, msel, strans, srecv,
    xsem, own_sem, ring_send, ring_recv, q_send, q_recv, o_send, o_recv, s_send, s_recv,
):
    n_row, n_col, rows, cols, cz, heads, rows_dev, selected = cfg
    head_dim = cz // heads
    per = selected // n_col
    half = n_row // 2
    first_half = rows_dev // 2
    MESH = pl.DeviceIdType.MESH
    r = lax.axis_index("row")
    c = lax.axis_index("col")

    def row_of(pos):
        pos = lax.rem(pos + 2 * n_row, n_row)
        return jnp.where(pos < half, 2 * pos, 2 * (n_row - 1 - pos) + 1)

    odd = lax.rem(r, 2)
    pos = jnp.where(odd == 0, r // 2, n_row - 1 - r // 2)
    nexts = (row_of(pos + 1), row_of(pos - 1))
    root = (r * rows) // cols
    start = pl.multiple_of(lax.rem(r * rows, cols), rows)
    is_root = c == root

    def x_copy(k):
        where = pl.ds(k * ROWS_CHUNK, ROWS_CHUNK)
        return pltpu.make_async_copy(pair_ref.at[where], xbuf.at[where], xsem.at[k])

    chunks = rows // ROWS_CHUNK
    for k in range(chunks):
        x_copy(k).start()
    own = pltpu.make_async_copy(nloc, nall.at[pl.ds(r * rows_dev, rows_dev)], own_sem)
    own.start()

    barrier = pltpu.get_barrier_semaphore()
    for nb in nexts:
        pl.semaphore_signal(barrier, inc=1, device_id=(nb, c), device_id_type=MESH)
    for dc in range(1, n_col):
        pl.semaphore_signal(
            barrier, inc=1, device_id=(r, lax.rem(c + dc, n_col)), device_id_type=MESH
        )
    pl.semaphore_wait(barrier, 2 + n_col - 1)

    def valid(way, s, u):
        if s < half:
            return True
        return s == half and ((u < first_half) if way == 0 else (u >= first_half))

    piece = cols // PIECES

    def ring(way, s, u, b):
        origin = row_of(pos - (s - 1) if way == 0 else pos + (s - 1))
        t = origin * rows_dev + u
        part = pl.ds(b * piece, piece)
        return pltpu.make_async_remote_copy(
            src_ref=nloc.at[u, part] if s == 1 else nall.at[t, part],
            dst_ref=nall.at[t, part],
            send_sem=ring_send.at[way],
            recv_sem=ring_recv.at[way, s - 1, u, b],
            device_id=(nexts[way], c),
            device_id_type=MESH,
        )

    def q_local(t):
        return pltpu.make_async_copy(nall.at[t, pl.ds(start, rows)], qn.at[t], q_recv.at[t])

    def q_remote(t, dc):
        return pltpu.make_async_remote_copy(
            src_ref=nall.at[t, pl.ds(start, rows)],
            dst_ref=qn.at[t],
            send_sem=q_send.at[dc - 1],
            recv_sem=q_recv.at[t],
            device_id=(r, lax.rem(c + dc, n_col)),
            device_id_type=MESH,
        )

    def q_share(t):
        @pl.when(is_root)
        def _():
            for dc in range(1, n_col):
                q_remote(t, dc).start()
            q_local(t).start()

    for u in range(rows_dev):
        for b in range(PIECES):
            for way in (0, 1):
                ring(way, 1, u, b).start()
    own.wait()
    for u in range(rows_dev):
        q_share(r * rows_dev + u)

    events = [
        [(way, s, u) for way in (0, 1) if valid(way, s, u)]
        for s in range(1, half + 1)
        for u in range(rows_dev)
    ]

    def token_row(way, s, u):
        return row_of(pos - s if way == 0 else pos + s) * rows_dev + u

    def arrive(group):
        for b in range(PIECES):
            for way, s, u in group:
                part = nall.at[token_row(way, s, u), pl.ds(b * piece, piece)]
                pltpu.make_async_remote_copy(
                    src_ref=part,
                    dst_ref=part,
                    send_sem=ring_send.at[way],
                    recv_sem=ring_recv.at[way, s - 1, u, b],
                    device_id=(nexts[way], c),
                    device_id_type=MESH,
                ).wait_recv()
                if valid(way, s + 1, u):
                    ring(way, s + 1, u, b).start()
        for way, s, u in group:
            q_share(token_row(way, s, u))

    row_i = lax.broadcasted_iota(jnp.int32, (cz, cz), 0)
    col_i = lax.broadcasted_iota(jnp.int32, (cz, cz), 1)
    centring = (jnp.where(row_i == col_i, 1.0, 0.0) - 1.0 / cz).astype(BF16)
    pick = lax.broadcasted_iota(jnp.int32, (16, heads), 0)
    head_i = lax.broadcasted_iota(jnp.int32, (16, heads), 1)
    pick = jnp.where((pick == head_i) | (pick == head_i + heads), 1.0, 0.0).astype(BF16)
    by_head = lax.dot_general(
        pick, wb_ref[...], (((1,), (0,)), ((), ())), preferred_element_type=F32
    )
    add = jnp.sum(by_head * shift_ref[...], axis=-1, keepdims=True)
    scaled = by_head * gain_ref[...]
    high = scaled.astype(BF16).astype(F32)
    line = lax.broadcasted_iota(jnp.int32, (16, cz), 0)
    left = jnp.concatenate(
        [
            jnp.where(line < heads, high, scaled - high),
            jnp.where(line == 2 * heads, F32(1.0 / cz), F32(0.0)),
        ],
        axis=-1,
    ).astype(BF16)

    def bias_step(j0):
        j0 = pl.multiple_of(j0, ROWS_STEP)
        x = xbuf[pl.ds(j0, ROWS_STEP)].reshape(ROWS_STEP * cols, cz)
        d = jnp.dot(x, centring, preferred_element_type=F32).astype(BF16)
        both = jnp.concatenate([d, d * d], axis=-1)
        res = lax.dot_general(
            left, both, (((1,), (1,)), ((), ())), preferred_element_type=F32
        )
        for jj in range(ROWS_STEP):
            at = pl.ds(pl.multiple_of((j0 + jj) * 16, 16), 16)
            for part in range(cols // 128):
                first = jj * cols + part * 128
                rbuf[part, at, :] = res[:, first : first + 128]

    for k in range(chunks):
        x_copy(k).wait()

        def one(b, _, k=k):
            bias_step(k * ROWS_CHUNK + b * ROWS_STEP)
            return 0

        lax.fori_loop(0, ROWS_CHUNK // ROWS_STEP, one, 0)
        if k == chunks // 2 - 1:
            arrive(events[0])
        if k == chunks * 3 // 4 - 1:
            arrive(events[1])

    for part in range(cols // 128):
        lanes = slice(part * 128, (part + 1) * 128)
        rstd = lax.rsqrt(rbuf[part, pl.ds(2 * heads, rows, stride=16), :] + 1e-05)
        live = mask_ref[:, lanes] > 0
        for h in range(heads):
            raw = (
                rbuf[part, pl.ds(h, rows, stride=16), :]
                + rbuf[part, pl.ds(heads + h, rows, stride=16), :]
            )
            full = raw * rstd + add[h : h + 1]
            bias[pl.ds(h * rows, rows), lanes] = jnp.where(live, full, F32(-1e9))

    lane = lax.broadcasted_iota(jnp.int32, (rows, cz), 1)
    in_head = [(lane // head_dim) == h for h in range(heads)]
    ones = jnp.ones((cols, cz), BF16)
    wkv = jnp.concatenate([wk_ref[...], wv_ref[...]], axis=-1)
    lsel[...] = jnp.ones_like(lsel)
    msel[...] = jnp.zeros_like(msel)
    scale = F32(1.0 / (head_dim ** 0.5))

    def o_copy(t, peer):
        return pltpu.make_async_remote_copy(
            src_ref=osend.at[t],
            dst_ref=orecv.at[c, lax.rem(t, per)],
            send_sem=o_send.at[peer],
            recv_sem=o_recv.at[c],
            device_id=(r, peer),
            device_id_type=MESH,
        )

    def attend(t, ls, ms):
        kv = jnp.dot(nall[t], wkv, preferred_element_type=F32).astype(BF16)
        key = kv[:, :cz]
        value = jnp.concatenate([kv[:, cz:], ones], axis=-1)
        q = (jnp.dot(qn[t], wq_ref[...], preferred_element_type=F32) * scale).astype(BF16)
        q4 = jnp.concatenate([jnp.where(in_head[h], q, jnp.zeros_like(q)) for h in range(heads)], 0)
        s = lax.dot_general(q4, key, (((1,), (1,)), ((), ())), preferred_element_type=F32)
        s = s + bias[...]
        m = jnp.max(s, axis=-1, keepdims=True)
        p = jnp.exp(s - m).astype(BF16)
        o = jnp.dot(p, value, preferred_element_type=F32)
        num = jnp.zeros((rows, cz), F32)
        den = jnp.zeros((rows, cz), F32)
        for h in range(heads):
            oh = o[h * rows : (h + 1) * rows, :cz]
            lh = o[h * rows : (h + 1) * rows, cz:]
            num = jnp.where(in_head[h], oh, num)
            den = jnp.where(in_head[h], lh, den)
            here = lane == t * heads + h
            ls = jnp.where(here, lh, ls)
            ms = jnp.where(here, m[h * rows : (h + 1) * rows], ms)
        osend[t] = (num / den).astype(BF16)
        return ls, ms

    def attend_group(rows_of):
        for t in rows_of:
            q_local(t).wait()
        ls = lsel[...]
        ms = msel[...]
        for t in rows_of:
            ls, ms = attend(t, ls, ms)
        lsel[...] = ls
        msel[...] = ms
        for t in rows_of:
            peer = t // per

            @pl.when(peer != c)
            def _(t=t, peer=peer):
                o_copy(t, peer).start()

    todo = [[r * rows_dev + u for u in range(rows_dev)]]
    todo += [[token_row(*e) for e in group] for group in events]
    done = 0
    for g in range(2, len(events)):
        arrive(events[g])
        upto = g - 1 if g < len(events) - 2 else g
        if g == len(events) - 1:
            upto = len(todo)
        if g == len(events) - 1:
            todo[-2:] = [todo[-2] + todo[-1]]
        for rows_of in todo[done:upto]:
            attend_group(rows_of)
        done = upto

    strans[...] = jnp.transpose(msel[...] + jnp.log(lsel[...]))
    ph = per * heads

    def s_copy(peer):
        return pltpu.make_async_remote_copy(
            src_ref=strans.at[pl.ds(pl.multiple_of(peer * ph, 8), ph)],
            dst_ref=srecv.at[pl.ds(pl.multiple_of(c * ph, 8), ph)],
            send_sem=s_send.at[peer],
            recv_sem=s_recv.at[c],
            device_id=(r, peer),
            device_id_type=MESH,
        )

    for dc in range(1, n_col):
        s_copy(lax.rem(c + dc, n_col)).start()
    own_rows = pl.ds(pl.multiple_of(c * ph, 8), ph)
    srecv[own_rows, :] = strans[own_rows, :]

    gates = []
    for i in range(per):
        g = jnp.dot(qn[c * per + i], wg_ref[...], preferred_element_type=F32) + gb_ref[...]
        gates.append(jax.nn.sigmoid(g).astype(BF16).astype(F32))
    span = selected * heads
    er = lax.broadcasted_iota(jnp.int32, (span, n_col * per * cz), 0)
    ec = lax.broadcasted_iota(jnp.int32, (span, n_col * per * cz), 1)
    expand = jnp.where(er == ec // head_dim, 1.0, 0.0).astype(BF16)

    for dc in range(1, n_col):
        src = lax.rem(c + dc, n_col)
        pltpu.make_async_remote_copy(
            src_ref=strans.at[pl.ds(0, ph)],
            dst_ref=srecv.at[pl.ds(pl.multiple_of(src * ph, 8), ph)],
            send_sem=s_send.at[src],
            recv_sem=s_recv.at[src],
            device_id=(r, src),
            device_id_type=MESH,
        ).wait_recv()
    stats = [srecv[pl.ds(k * ph, ph), :] for k in range(n_col)]
    top = functools.reduce(jnp.maximum, stats)
    weights = [jnp.exp(a - top) for a in stats]
    total = functools.reduce(jnp.add, weights)
    parts = jnp.concatenate([w / total for w in weights], axis=0)
    spread_w = jnp.dot(jnp.transpose(parts).astype(BF16), expand, preferred_element_type=F32)

    for dc in range(1, n_col):
        src = lax.rem(c + dc, n_col)
        pltpu.make_async_remote_copy(
            src_ref=osend.at[pl.ds(0, per)],
            dst_ref=orecv.at[src],
            send_sem=o_send.at[src],
            recv_sem=o_recv.at[src],
            device_id=(r, src),
            device_id_type=MESH,
        ).wait_recv()
    for i in range(per):
        orecv[c, i] = osend[c * per + i]
    for i in range(per):
        acc = jnp.zeros((rows, cz), F32)
        for k in range(n_col):
            at = (k * per + i) * cz
            acc = acc + spread_w[:, at : at + cz] * orecv[k, i].astype(F32)
        gated = (gates[i] * acc).astype(BF16)
        out_ref[i] = jnp.dot(gated, wo_ref[...], preferred_element_type=F32).astype(BF16)

    for dc in range(1, n_col):
        peer = lax.rem(c + dc, n_col)
        s_copy(peer).wait_send()
        pltpu.make_async_remote_copy(
            src_ref=osend.at[pl.ds(0, per)],
            dst_ref=orecv.at[c],
            send_sem=o_send.at[peer],
            recv_sem=o_recv.at[c],
            device_id=(r, peer),
            device_id_type=MESH,
        ).wait_send()

        @pl.when(is_root)
        def _(dc=dc):
            pltpu.make_async_remote_copy(
                src_ref=qn,
                dst_ref=qn,
                send_sem=q_send.at[dc - 1],
                recv_sem=q_recv.at[0],
                device_id=(r, lax.rem(c + dc, n_col)),
                device_id_type=MESH,
            ).wait_send()

    for way in (0, 1):
        count = sum(valid(way, s, u) for s in range(1, half + 1) for u in range(rows_dev))
        pltpu.make_async_remote_copy(
            src_ref=nall.at[pl.ds(0, count)],
            dst_ref=nall.at[pl.ds(0, count)],
            send_sem=ring_send.at[way],
            recv_sem=ring_recv.at[way, 0, 0, 0],
            device_id=(nexts[way], c),
            device_id_type=MESH,
        ).wait_send()


def body(
    pair_rep, row_ids, pad_mask, ln_gain, ln_bias, w_query, w_key, w_value, w_gate, gate_bias,
    w_bias, w_out,
):
    rows, cols, cz = pair_rep.shape
    heads = w_bias.shape[1]
    n_row = lax.axis_size("row")
    n_col = lax.axis_size("col")
    rows_dev = row_ids.shape[0]
    selected = rows_dev * n_row
    per = selected // n_col
    half = n_row // 2
    nloc = chosen_normed(pair_rep, row_ids, ln_gain[None], ln_bias[None])
    cfg = (n_row, n_col, rows, cols, cz, heads, rows_dev, selected)
    DMA = pltpu.SemaphoreType.DMA
    return pl.pallas_call(
        functools.partial(main_kernel, cfg),
        out_shape=jax.ShapeDtypeStruct((per, rows, cz), BF16),
        in_specs=[pl.BlockSpec(memory_space=pl.ANY)] + [VM] * 11,
        out_specs=VM,
        scratch_shapes=[
            pltpu.VMEM((rows, cols, cz), BF16),
            pltpu.VMEM((cols // 128, rows * 16, 128), F32),
            pltpu.VMEM((heads * rows, cols), F32),
            pltpu.VMEM((selected, cols, cz), BF16),
            pltpu.VMEM((selected, rows, cz), BF16),
            pltpu.VMEM((selected, rows, cz), BF16),
            pltpu.VMEM((n_col, per, rows, cz), BF16),
            pltpu.VMEM((rows, cz), F32),
            pltpu.VMEM((rows, cz), F32),
            pltpu.VMEM((cz, rows), F32),
            pltpu.VMEM((selected * heads, rows), F32),
            DMA((rows // ROWS_CHUNK,)),
            DMA,
            DMA((2,)),
            DMA((2, half, rows_dev, PIECES)),
            DMA((n_col - 1,)),
            DMA((selected,)),
            DMA((n_col,)),
            DMA((n_col,)),
            DMA((n_col,)),
            DMA((n_col,)),
        ],
        compiler_params=pltpu.CompilerParams(
            collective_id=0, has_side_effects=True, vmem_limit_bytes=56 * 2**20
        ),
    )(
        pair_rep, nloc, pad_mask[None], ln_gain[None], ln_bias[None], w_bias.T, w_query, w_key,
        w_value, w_gate, gate_bias[None], w_out,
    )


def solution(mesh):
    return jax.shard_map(
        body,
        mesh=mesh,
        in_specs=(P("row", "col", None), P("row"), P("col")) + (P(),) * 9,
        out_specs=P("col", "row", None),
        check_vma=False,
    )
```
